32 devices in a mesh: vox: 4 (over x, core), var: 8 (over z, y).
Axes of the slice: x: 2, y: 2, z: 4, core: 2. Of those that a mesh axis runs over, the one named last changes fastest.
Arguments:
- cross: float32 [16384, 24576], P('vox', 'var')
- start: float32 [32, 24576], P(None, 'var'), may hold values from -6 to 6
- levels: int32 [2, 32], replicated, may hold values from 0 to 767, as said below
Outputs:
- deflated: float32 [16384, 24576], P('vox', 'var')
- left_dirs: float32 [32, 16384], P(None, 'vox')
- right_dirs: float32 [32, 24576], P(None, 'var')
- strength: float32 [32], replicated
The draws below stay inside these ranges and needn't reach their ends.
Inputs may be any that keep to these rules, and one draw needn't show every extreme that they name: `levels`: both 0 and 767 occur in every draw.
All inputs are finite; a program needn't handle non-finite values.
Results may differ from the reference program's by a relative error of at most 0.0003.
Values sent between devices are 32-bit elements; how exact they have to be, the bound alone decides.
A program may use at most 192 MiB of HBM per device.

```python
import math
import jax
import jax.numpy as jnp
from jax import lax

NV = 16384
NG = 24576
K = 32
ITERS = 2


def draw_cross(key, part):
    keys = jax.random.split(jax.random.fold_in(key, 7), 3)
    ramp_rows = 1.0 + 2.0 * jnp.arange(NV, dtype=jnp.float32) / NV
    ramp_cols = 1.0 + 2.0 * jnp.arange(NG, dtype=jnp.float32) / NG
    row_scale = jnp.exp(jax.random.uniform(keys[0], (NV,), jnp.float32, 0.0, math.log(10.0))) * ramp_rows / 5.0
    col_scale = jnp.exp(jax.random.uniform(keys[1], (NG,), jnp.float32, 0.0, math.log(10.0))) * ramp_cols / 5.0
    noise = jax.random.normal(keys[2], (NV, NG), jnp.float32)
    return noise * row_scale[:, None] * col_scale[None, :]


def draw_levels(key, part):
    keys = jax.random.split(jax.random.fold_in(key, 11), 3)
    values = jax.random.randint(keys[0], (2 * K,), 0, 768)
    high_pos = jax.random.randint(keys[1], (), 0, 2 * K)
    low_pos = (high_pos + 1 + jax.random.randint(keys[2], (), 0, 2 * K - 1)) % (2 * K)
    where_idx = jnp.arange(2 * K)
    values = jnp.where(where_idx == high_pos, 767, values)
    values = jnp.where(where_idx == low_pos, 0, values)
    return values.reshape(2, K).astype(jnp.int32)


def steps_of(stream_key, extent, cuts, smallest, high):
    def one(axis_at, shards_of):
        draws = jax.random.uniform(jax.random.fold_in(jax.random.fold_in(stream_key, 6), axis_at), (shards_of,), jnp.float32, smallest / len(cuts), high / len(cuts))
        return jnp.repeat(jnp.exp(draws), extent[axis_at] // shards_of).reshape((-1,) + (1,) * (len(extent) - axis_at - 1))

    level = one(*cuts[0])
    for cut in cuts[1:]:
        level = level * one(*cut)
    return level


def normal_values(own_key, shape, deviation, bound, cuts=(), held_as=jnp.bfloat16):
    result = deviation * jax.random.normal(own_key, shape, jnp.float32)
    if cuts:
        result = result * steps_of(own_key, shape, cuts, -0.22, 0.18)
    return jnp.clip(result, -bound, bound).astype(held_as)


def setup_inputs(seed: int = 0) -> dict:
    arg_keys = jax.random.split(jax.random.key(seed), 4)
    cross = draw_cross(jax.random.fold_in(arg_keys[3], 71), 0)
    start = normal_values(arg_keys[1], (K, NG), 1.0, 6.0, ((1, 8),), jnp.float32)
    levels = draw_levels(jax.random.fold_in(arg_keys[3], 71), 0)
    return dict(cross=cross, start=start, levels=levels)


EPSILON = 1e-06
HIGH = lax.Precision.HIGHEST

def shrink(values, thresholds, mean_sq):
    level = (thresholds * jnp.sqrt(mean_sq + EPSILON))[:, None]
    return values - jnp.clip(values, -level, level)

def orthonormal(shrunk, count):
    gram = lax.dot_general(shrunk.astype(jnp.float32), shrunk.astype(jnp.float32), (((1,), (1,)), ((), ())), precision=HIGH, preferred_element_type=jnp.float32)
    gram = gram / count + EPSILON * jnp.eye(gram.shape[0], dtype=jnp.float32)
    factor = jnp.linalg.cholesky(gram)
    return jax.scipy.linalg.solve_triangular(factor, shrunk, lower=True)

def reference(cross, start, levels):
    thresholds = levels.astype(jnp.float32) / 1024.0
    right_dirs = start
    left_dirs = None
    for sweep in range(ITERS):
        summed = lax.dot_general(right_dirs.astype(jnp.float32), cross.astype(jnp.float32), (((1,), (1,)), ((), ())), precision=HIGH, preferred_element_type=jnp.float32)
        shrunk = shrink(summed, thresholds[0], lax.optimization_barrier(jnp.sum(summed * summed, 1)) / NV)
        left_dirs = orthonormal(shrunk, NV)
        summed = jnp.dot(left_dirs.astype(jnp.float32), cross.astype(jnp.float32), precision=HIGH, preferred_element_type=jnp.float32)
        shrunk = shrink(summed, thresholds[1], lax.optimization_barrier(jnp.sum(summed * summed, 1)) / NG)
        right_dirs = orthonormal(shrunk, NG)
    projected = lax.dot_general(right_dirs.astype(jnp.float32), cross.astype(jnp.float32), (((1,), (1,)), ((), ())), precision=HIGH, preferred_element_type=jnp.float32)
    strength = lax.optimization_barrier(jnp.sum(left_dirs * projected, 1)) / math.sqrt(NV * NG)
    scaled = left_dirs * (strength / math.sqrt(NV * NG))[:, None]
    block_size = math.gcd(NV, 1024)
    nblocks = NV // block_size
    cross_blocks = cross.reshape(nblocks, block_size, NG)
    scaled_blocks = scaled.reshape(K, nblocks, block_size).transpose(1, 0, 2)

    def deflate_block(pair):
        block_rows, block_scaled = pair
        removed = lax.dot_general(block_scaled.astype(jnp.float32), right_dirs.astype(jnp.float32), (((0,), (0,)), ((), ())), precision=HIGH, preferred_element_type=jnp.float32)
        return block_rows - removed
    deflated = lax.map(deflate_block, (cross_blocks, scaled_blocks)).reshape(NV, NG)
    return (deflated, left_dirs, right_dirs, strength)
```

```python
import functools
import math

import jax
import jax.numpy as jnp
from jax import lax
from jax.experimental import pallas as pl
from jax.experimental.pallas import tpu as pltpu
from jax.sharding import PartitionSpec as P

ITERS = 2
EPSILON = 1e-06
HIGH = lax.Precision.HIGHEST
MESH = pl.DeviceIdType.MESH
F32 = jnp.float32
BF16 = jnp.bfloat16
LANES = 128
ROWS = 512
COLUMNS = 384


def halves(values):
    high = values.astype(BF16)
    return high, (values - high.astype(F32)).astype(BF16)


def block_rows(rows):
    return math.gcd(rows, ROWS)


def left_kernel(chunk, dirs_ref, cross_ref, out_ref, stacked):
    k = dirs_ref.shape[0]

    @pl.when(pl.program_id(0) == 0)
    def _():
        high, low = halves(dirs_ref[...])
        stacked[:k, :] = high
        stacked[k:, :] = low

    high, low = halves(cross_ref[...])
    dims = (((1,), (1,)), ((), ()))
    total = lax.dot_general(high, stacked[...], dims, preferred_element_type=F32)
    total = total + lax.dot_general(low, stacked[...], dims, preferred_element_type=F32)
    total = total.T
    total = total[:k] + total[k:]
    for at in range(out_ref.shape[0]):
        out_ref[at] = total[:, at * chunk : (at + 1) * chunk]


def left_pass(cross, dirs, chunk):
    rows, cols = cross.shape
    k = dirs.shape[0]
    size = block_rows(rows)
    size = max(size, chunk)
    return pl.pallas_call(
        functools.partial(left_kernel, chunk),
        out_shape=jax.ShapeDtypeStruct((rows // chunk, k, chunk), F32),
        grid=(rows // size,),
        in_specs=[
            pl.BlockSpec((k, cols), lambda i: (0, 0)),
            pl.BlockSpec((size, cols), lambda i: (i, 0)),
        ],
        out_specs=pl.BlockSpec((size // chunk, k, chunk), lambda i: (i, 0, 0)),
        scratch_shapes=[pltpu.VMEM((2 * k, cols), BF16)],
        name="left_pass",
    )(dirs, cross)


def right_kernel(dirs_ref, cross_ref, out_ref, stacked):
    k = dirs_ref.shape[0]

    @pl.when(pl.program_id(0) == 0)
    def _():
        high, low = halves(dirs_ref[...])
        stacked[:k, :] = high
        stacked[k:, :] = low

    high, low = halves(cross_ref[...])
    total = jnp.dot(stacked[...], high, preferred_element_type=F32)
    total = total + jnp.dot(stacked[...], low, preferred_element_type=F32)
    out_ref[0] = total[:k] + total[k:]


def right_pass(cross, dirs, chunk):
    rows, cols = cross.shape
    k = dirs.shape[0]
    size = math.gcd(chunk, COLUMNS)
    per = chunk // size
    return pl.pallas_call(
        right_kernel,
        out_shape=jax.ShapeDtypeStruct((cols // chunk, k, chunk), F32),
        grid=(cols // size,),
        in_specs=[
            pl.BlockSpec((k, rows), lambda j: (0, 0)),
            pl.BlockSpec((rows, size), lambda j: (0, j)),
        ],
        out_specs=pl.BlockSpec((1, k, size), lambda j: (j // per, 0, j % per)),
        scratch_shapes=[pltpu.VMEM((2 * k, rows), BF16)],
        name="right_pass",
    )(dirs, cross)


def deflate_kernel(left_ref, scale_ref, right_ref, cross_ref, out_ref, stacked):
    k = right_ref.shape[0]

    @pl.when(pl.program_id(0) == 0)
    def _():
        high, low = halves(right_ref[...])
        stacked[:k, :] = high
        stacked[k : 2 * k, :] = high
        stacked[2 * k :, :] = low

    high, low = halves(left_ref[...] * scale_ref[:, :1])
    scaled = jnp.concatenate([high, low, high], axis=0)
    removed = lax.dot_general(
        scaled, stacked[...], (((0,), (0,)), ((), ())), preferred_element_type=F32
    )
    out_ref[...] = cross_ref[...] - removed


def deflate(cross, left_dirs, scale, right_dirs):
    rows, cols = cross.shape
    k = left_dirs.shape[0]
    size = block_rows(rows)
    return pl.pallas_call(
        deflate_kernel,
        out_shape=jax.ShapeDtypeStruct((rows, cols), F32),
        grid=(rows // size,),
        in_specs=[
            pl.BlockSpec((k, size), lambda i: (0, i)),
            pl.BlockSpec((k, LANES), lambda i: (0, 0)),
            pl.BlockSpec((k, cols), lambda i: (0, 0)),
            pl.BlockSpec((size, cols), lambda i: (i, 0)),
        ],
        out_specs=pl.BlockSpec((size, cols), lambda i: (i, 0)),
        scratch_shapes=[pltpu.VMEM((3 * k, cols), BF16)],
        name="deflate",
    )(left_dirs, scale, right_dirs, cross)


def inverse_factor(gram):
    k = gram.shape[0]
    row = lax.broadcasted_iota(jnp.int32, gram.shape, 0)
    lane = lax.broadcasted_iota(jnp.int32, gram.shape, 1)
    table = jnp.where(lane < k, gram, jnp.where(lane == row + k, 1.0, 0.0))
    below = row[:, :1]
    for at in range(k - 1):
        pivot = table[at : at + 1, :]
        column = table[:, at : at + 1]
        factor = jnp.where(below > at, column / pivot[:, at : at + 1], 0.0)
        table = table - factor * pivot
    diag = jnp.sum(jnp.where(lane == row, table, 0.0), axis=1, keepdims=True)
    return pltpu.roll(table / jnp.sqrt(diag), LANES - k, 1)[:, :k]


def pack(table):
    k = table.shape[0]
    rows = k * k // LANES
    group = lax.broadcasted_iota(jnp.int32, (rows, LANES), 1) // k
    packed = table[:rows]
    for at in range(1, LANES // k):
        packed = jnp.where(group == at, table[at * rows : (at + 1) * rows], packed)
    return packed


def unpack(packed, k):
    pieces = [packed]
    for at in range(1, LANES // k):
        pieces.append(pltpu.roll(packed, LANES - at * k, 1))
    return jnp.concatenate(pieces, axis=0)


def exchange(table, count, axis, me, sends, recvs):
    copies = []
    for hop in range(1, count):
        other = lax.rem(me + hop, count)
        copy = pltpu.make_async_remote_copy(
            src_ref=table.at[me],
            dst_ref=table.at[me],
            send_sem=sends.at[hop - 1],
            recv_sem=recvs.at[hop - 1],
            device_id={axis: other},
            device_id_type=MESH,
        )
        copy.start()
        copies.append(copy)
    return copies


def orth_kernel(axis, parts, other_axis, others, count, final, part_ref, thr_ref, *refs):
    outs, refs = refs[: 2 if final else 1], refs[2 if final else 1 :]
    landed, gathered, squares, grams, rs_s, rs_r, ag_s, ag_r, sq_s, sq_r, gr_s, gr_r = refs
    dirs_ref = outs[0]
    pieces, k, chunk = part_ref.shape
    me = lax.axis_index(axis)
    mine = lax.axis_index(other_axis)

    barrier = pltpu.get_barrier_semaphore()
    for hop in range(1, parts):
        pl.semaphore_signal(
            barrier, inc=1, device_id={axis: lax.rem(me + hop, parts)}, device_id_type=MESH
        )
    for hop in range(1, others):
        pl.semaphore_signal(
            barrier, inc=1, device_id={other_axis: lax.rem(mine + hop, others)}, device_id_type=MESH
        )
    pl.semaphore_wait(barrier, parts + others - 2)

    if parts > 1:
        first = []
        for hop in range(1, parts):
            other = lax.rem(me + hop, parts)
            copy = pltpu.make_async_remote_copy(
                src_ref=part_ref.at[other],
                dst_ref=landed.at[hop - 1],
                send_sem=rs_s.at[hop - 1],
                recv_sem=rs_r.at[hop - 1],
                device_id={axis: other},
                device_id_type=MESH,
            )
            copy.start()
            first.append(copy)
        total = part_ref[me]
        for hop in range(1, parts):
            first[hop - 1].wait()
            total = total + landed[hop - 1]
        gathered[me] = total
        for copy in exchange(gathered, parts, axis, me, ag_s, ag_r):
            copy.wait()
    else:
        gathered[...] = part_ref[...]

    sums = jnp.zeros((k, chunk), F32)
    for at in range(pieces):
        values = gathered[at]
        sums = sums + values * values
    squares[mine] = pack(jnp.broadcast_to(jnp.sum(sums, axis=1, keepdims=True), (k, LANES)))
    for copy in exchange(squares, others, other_axis, mine, sq_s, sq_r):
        copy.wait()
    mean = squares[0]
    for at in range(1, others):
        mean = mean + squares[at]
    mean = unpack(mean, k)
    level = (thr_ref[...] * jnp.sqrt(mean / count + EPSILON))[:, :1]

    gram = jnp.zeros((2 * k if final else k, LANES), F32)
    shrunk = []
    for at in range(pieces):
        values = gathered[at]
        short = values - jnp.clip(values, -level, level)
        shrunk.append(short)
        against = jnp.concatenate([short] * (LANES // k), axis=0)
        rows = jnp.concatenate([short, values], axis=0) if final else short
        gram = gram + lax.dot_general(
            rows, against, (((1,), (1,)), ((), ())), precision=HIGH, preferred_element_type=F32
        )
    half = squares.shape[1]
    if final:
        grams[mine] = jnp.concatenate([pack(gram[:k]), pack(gram[k:])], axis=0)
    else:
        grams[mine] = pack(gram)
    for copy in exchange(grams, others, other_axis, mine, gr_s, gr_r):
        copy.wait()
    gram = grams[0]
    for at in range(1, others):
        gram = gram + grams[at]
    cross_gram = unpack(gram[half:], k) if final else None
    gram = unpack(gram[:half], k)
    row = lax.broadcasted_iota(jnp.int32, (k, LANES), 0)
    lane = lax.broadcasted_iota(jnp.int32, (k, LANES), 1)
    inverse = inverse_factor(gram / count + jnp.where(row == lane, EPSILON, 0.0))
    for at in range(pieces):
        dirs_ref[:, at * chunk : (at + 1) * chunk] = jnp.dot(
            inverse, shrunk[at], precision=HIGH, preferred_element_type=F32
        )
    if final:
        strength = jnp.sum(cross_gram[:, :k] * inverse, axis=1, keepdims=True)
        outs[1][...] = jnp.broadcast_to(strength, (k, LANES))


def orth_step(partial, thresholds, axis, parts, other_axis, others, count, ident, final=False):
    pieces, k, chunk = partial.shape
    if pieces != parts:
        partial = lax.psum(partial, axis)
        parts = 1
    slots = max(parts - 1, 1)
    dma = pltpu.SemaphoreType.DMA
    vmem = pl.BlockSpec(memory_space=pltpu.VMEM)
    out_shape = [jax.ShapeDtypeStruct((k, pieces * chunk), F32)]
    if final:
        out_shape.append(jax.ShapeDtypeStruct((k, LANES), F32))
    return pl.pallas_call(
        functools.partial(orth_kernel, axis, parts, other_axis, others, count, final),
        out_shape=out_shape,
        in_specs=[vmem, vmem],
        out_specs=[vmem] * len(out_shape),
        scratch_shapes=[
            pltpu.VMEM((slots, k, chunk), F32),
            pltpu.VMEM((pieces, k, chunk), F32),
            pltpu.VMEM((others, k * k // LANES, LANES), F32),
            pltpu.VMEM((others, (2 if final else 1) * k * k // LANES, LANES), F32),
            dma((slots,)),
            dma((slots,)),
            dma((slots,)),
            dma((slots,)),
            dma((others - 1,)),
            dma((others - 1,)),
            dma((others - 1,)),
            dma((others - 1,)),
        ],
        compiler_params=pltpu.CompilerParams(collective_id=ident, has_side_effects=True),
        name=f"orth_{ident}",
    )(partial, thresholds)


def chunk_of(size, parts):
    chunk = size // parts
    return chunk if chunk * parts == size and chunk % LANES == 0 else size


def solution(mesh):
    vox, var = mesh.shape["vox"], mesh.shape["var"]

    def per_device(cross, start, levels):
        rows, cols = cross.shape
        k = start.shape[0]
        nv, ng = rows * vox, cols * var
        thresholds = levels.astype(F32) / 1024.0
        thresholds = jnp.broadcast_to(thresholds[:, :, None], (2, k, LANES))
        row_chunk, col_chunk = chunk_of(rows, var), chunk_of(cols, vox)
        right_dirs = start
        for sweep in range(ITERS):
            final = sweep == ITERS - 1
            partial = left_pass(cross, right_dirs, row_chunk)
            left_dirs = orth_step(partial, thresholds[0], "var", var, "vox", vox, nv, 2 * sweep)[0]
            partial = right_pass(cross, left_dirs, col_chunk)
            outs = orth_step(
                partial, thresholds[1], "vox", vox, "var", var, ng, 2 * sweep + 1, final
            )
            right_dirs = outs[0]
        root = math.sqrt(nv * ng)
        strength = outs[1] / root
        deflated = deflate(cross, left_dirs, strength / root, right_dirs)
        return (deflated, left_dirs, right_dirs, strength[:, 0])

    in_specs = (P("vox", "var"), P(None, "var"), P())
    out_specs = (P("vox", "var"), P(None, "vox"), P(None, "var"), P())
    return jax.shard_map(
        per_device, mesh=mesh, in_specs=in_specs, out_specs=out_specs, check_vma=False
    )
```

```python
import functools
import math

import jax
import jax.numpy as jnp
from jax import lax
from jax.experimental import pallas as pl
from jax.experimental.pallas import tpu as pltpu
from jax.sharding import PartitionSpec as P

ITERS = 2
EPSILON = 1e-06
MESH = pl.DeviceIdType.MESH
F32 = jnp.float32
BF16 = jnp.bfloat16
LANES = 128
ROWS = 512
COLUMNS = 384


def halves(values):
    high = values.astype(BF16)
    return high, (values - high.astype(F32)).astype(BF16)


def block_rows(rows):
    return math.gcd(rows, ROWS)


def left_kernel(chunk, dirs_ref, cross_ref, out_ref, stacked):
    k = dirs_ref.shape[0]

    @pl.when(pl.program_id(0) == 0)
    def _():
        high, low = halves(dirs_ref[...])
        stacked[:k, :] = high
        stacked[k:, :] = low

    high, low = halves(cross_ref[...])
    dims = (((1,), (1,)), ((), ()))
    total = lax.dot_general(high, stacked[...], dims, preferred_element_type=F32)
    total = total + lax.dot_general(low, stacked[...], dims, preferred_element_type=F32)
    total = total.T
    total = total[:k] + total[k:]
    for at in range(out_ref.shape[0]):
        out_ref[at] = total[:, at * chunk : (at + 1) * chunk]


def left_pass(cross, dirs, chunk):
    rows, cols = cross.shape
    k = dirs.shape[0]
    size = block_rows(rows)
    size = max(size, chunk)
    return pl.pallas_call(
        functools.partial(left_kernel, chunk),
        out_shape=jax.ShapeDtypeStruct((rows // chunk, k, chunk), F32),
        grid=(rows // size,),
        in_specs=[
            pl.BlockSpec((k, cols), lambda i: (0, 0)),
            pl.BlockSpec((size, cols), lambda i: (i, 0)),
        ],
        out_specs=pl.BlockSpec((size // chunk, k, chunk), lambda i: (i, 0, 0)),
        scratch_shapes=[pltpu.VMEM((2 * k, cols), BF16)],
        name="left_pass",
    )(dirs, cross)


def right_kernel(dirs_ref, cross_ref, out_ref, stacked):
    k = dirs_ref.shape[0]

    @pl.when(pl.program_id(0) == 0)
    def _():
        high, low = halves(dirs_ref[...])
        stacked[:k, :] = high
        stacked[k:, :] = low

    high, low = halves(cross_ref[...])
    total = jnp.dot(stacked[...], high, preferred_element_type=F32)
    total = total + jnp.dot(stacked[...], low, preferred_element_type=F32)
    out_ref[0] = total[:k] + total[k:]


def right_pass(cross, dirs, chunk):
    rows, cols = cross.shape
    k = dirs.shape[0]
    size = math.gcd(chunk, COLUMNS)
    per = chunk // size
    return pl.pallas_call(
        right_kernel,
        out_shape=jax.ShapeDtypeStruct((cols // chunk, k, chunk), F32),
        grid=(cols // size,),
        in_specs=[
            pl.BlockSpec((k, rows), lambda j: (0, 0)),
            pl.BlockSpec((rows, size), lambda j: (0, j)),
        ],
        out_specs=pl.BlockSpec((1, k, size), lambda j: (j // per, 0, j % per)),
        scratch_shapes=[pltpu.VMEM((2 * k, rows), BF16)],
        name="right_pass",
    )(dirs, cross)


def deflate_kernel(left_ref, scale_ref, right_ref, cross_ref, out_ref, stacked):
    k = right_ref.shape[0]

    @pl.when(pl.program_id(0) == 0)
    def _():
        high, low = halves(right_ref[...])
        stacked[:k, :] = high
        stacked[k : 2 * k, :] = high
        stacked[2 * k :, :] = low

    high, low = halves(left_ref[...] * scale_ref[:, :1])
    scaled = jnp.concatenate([high, low, high], axis=0)
    removed = lax.dot_general(
        scaled, stacked[...], (((0,), (0,)), ((), ())), preferred_element_type=F32
    )
    out_ref[...] = cross_ref[...] - removed


def deflate(cross, left_dirs, scale, right_dirs):
    rows, cols = cross.shape
    k = left_dirs.shape[0]
    size = block_rows(rows)
    return pl.pallas_call(
        deflate_kernel,
        out_shape=jax.ShapeDtypeStruct((rows, cols), F32),
        grid=(rows // size,),
        in_specs=[
            pl.BlockSpec((k, size), lambda i: (0, i)),
            pl.BlockSpec((k, LANES), lambda i: (0, 0)),
            pl.BlockSpec((k, cols), lambda i: (0, 0)),
            pl.BlockSpec((size, cols), lambda i: (i, 0)),
        ],
        out_specs=pl.BlockSpec((size, cols), lambda i: (i, 0)),
        scratch_shapes=[pltpu.VMEM((3 * k, cols), BF16)],
        name="deflate",
    )(left_dirs, scale, right_dirs, cross)


def inverse_factor(gram):
    k = gram.shape[0]
    row = lax.broadcasted_iota(jnp.int32, gram.shape, 0)
    lane = lax.broadcasted_iota(jnp.int32, gram.shape, 1)
    table = jnp.where(lane < k, gram, jnp.where(lane == row + k, 1.0, 0.0))
    below = row[:, :1]
    for at in range(k - 1):
        pivot = table[at : at + 1, :]
        column = table[:, at : at + 1]
        factor = jnp.where(below > at, column / pivot[:, at : at + 1], 0.0)
        table = table - factor * pivot
    diag = jnp.sum(jnp.where(lane == row, table, 0.0), axis=1, keepdims=True)
    return pltpu.roll(table / jnp.sqrt(diag), LANES - k, 1)[:, :k]


def pack(table):
    k = table.shape[0]
    rows = k * k // LANES
    group = lax.broadcasted_iota(jnp.int32, (rows, LANES), 1) // k
    packed = table[:rows]
    for at in range(1, LANES // k):
        packed = jnp.where(group == at, table[at * rows : (at + 1) * rows], packed)
    return packed


def unpack(packed, k):
    pieces = [packed]
    for at in range(1, LANES // k):
        pieces.append(pltpu.roll(packed, LANES - at * k, 1))
    return jnp.concatenate(pieces, axis=0)


def exchange(table, count, axis, me, sends, recvs):
    copies = []
    for hop in range(1, count):
        other = lax.rem(me + hop, count)
        copy = pltpu.make_async_remote_copy(
            src_ref=table.at[me],
            dst_ref=table.at[me],
            send_sem=sends.at[hop - 1],
            recv_sem=recvs.at[hop - 1],
            device_id={axis: other},
            device_id_type=MESH,
        )
        copy.start()
        copies.append(copy)
    return copies


def orth_kernel(axis, parts, other_axis, others, count, final, part_ref, thr_ref, *refs):
    outs, refs = refs[: 2 if final else 1], refs[2 if final else 1 :]
    landed, gathered, squares, grams, rs_s, rs_r, ag_s, ag_r, sq_s, sq_r, gr_s, gr_r = refs
    dirs_ref = outs[0]
    pieces, k, chunk = part_ref.shape
    me = lax.axis_index(axis)
    mine = lax.axis_index(other_axis)

    barrier = pltpu.get_barrier_semaphore()
    for hop in range(1, parts):
        pl.semaphore_signal(
            barrier, inc=1, device_id={axis: lax.rem(me + hop, parts)}, device_id_type=MESH
        )
    for hop in range(1, others):
        pl.semaphore_signal(
            barrier, inc=1, device_id={other_axis: lax.rem(mine + hop, others)}, device_id_type=MESH
        )
    pl.semaphore_wait(barrier, parts + others - 2)

    if parts > 1:
        first = []
        for hop in range(1, parts):
            other = lax.rem(me + hop, parts)
            copy = pltpu.make_async_remote_copy(
                src_ref=part_ref.at[other],
                dst_ref=landed.at[hop - 1],
                send_sem=rs_s.at[hop - 1],
                recv_sem=rs_r.at[hop - 1],
                device_id={axis: other},
                device_id_type=MESH,
            )
            copy.start()
            first.append(copy)
        total = part_ref[me]
        for hop in range(1, parts):
            first[hop - 1].wait()
            total = total + landed[hop - 1]
        gathered[me] = total
        for copy in exchange(gathered, parts, axis, me, ag_s, ag_r):
            copy.wait()
    else:
        gathered[...] = part_ref[...]

    sums = jnp.zeros((k, chunk), F32)
    for at in range(pieces):
        values = gathered[at]
        sums = sums + values * values
    squares[mine] = pack(jnp.broadcast_to(jnp.sum(sums, axis=1, keepdims=True), (k, LANES)))
    for copy in exchange(squares, others, other_axis, mine, sq_s, sq_r):
        copy.wait()
    mean = squares[0]
    for at in range(1, others):
        mean = mean + squares[at]
    mean = unpack(mean, k)
    level = (thr_ref[...] * jnp.sqrt(mean / count + EPSILON))[:, :1]

    gram = jnp.zeros((2 * k if final else k, k), F32)
    shrunk = []
    dims = (((1,), (1,)), ((), ()))
    for at in range(pieces):
        values = gathered[at]
        high, low = halves(values - jnp.clip(values, -level, level))
        shrunk.append((high, low))
        rows = [high, low]
        tops = high
        if final:
            rows += list(halves(values))
            tops = jnp.concatenate([high, rows[2]], axis=0)
        rows = jnp.concatenate(rows, axis=0)
        wide = lax.dot_general(rows, high, dims, preferred_element_type=F32)
        part = wide[:k] + wide[k : 2 * k]
        if final:
            part = jnp.concatenate([part, wide[2 * k : 3 * k] + wide[3 * k :]], axis=0)
        gram = gram + (part + lax.dot_general(tops, low, dims, preferred_element_type=F32))
    gram = jnp.concatenate([gram] * (LANES // k), axis=1)
    half = squares.shape[1]
    if final:
        grams[mine] = jnp.concatenate([pack(gram[:k]), pack(gram[k:])], axis=0)
    else:
        grams[mine] = pack(gram)
    for copy in exchange(grams, others, other_axis, mine, gr_s, gr_r):
        copy.wait()
    gram = grams[0]
    for at in range(1, others):
        gram = gram + grams[at]
    cross_gram = unpack(gram[half:], k) if final else None
    gram = unpack(gram[:half], k)
    row = lax.broadcasted_iota(jnp.int32, (k, LANES), 0)
    lane = lax.broadcasted_iota(jnp.int32, (k, LANES), 1)
    inverse = inverse_factor(gram / count + jnp.where(row == lane, EPSILON, 0.0))
    top, rest = halves(inverse)
    stacked = jnp.concatenate([top, rest], axis=0)
    for at in range(pieces):
        high, low = shrunk[at]
        wide = jnp.dot(stacked, high, preferred_element_type=F32)
        last = jnp.dot(top, low, preferred_element_type=F32)
        dirs_ref[:, at * chunk : (at + 1) * chunk] = wide[:k] + (wide[k:] + last)
    if final:
        strength = jnp.sum(cross_gram[:, :k] * inverse, axis=1, keepdims=True)
        outs[1][...] = jnp.broadcast_to(strength, (k, LANES))


def orth_step(partial, thresholds, axis, parts, other_axis, others, count, ident, final=False):
    pieces, k, chunk = partial.shape
    if pieces != parts:
        partial = lax.psum(partial, axis)
        parts = 1
    slots = max(parts - 1, 1)
    dma = pltpu.SemaphoreType.DMA
    vmem = pl.BlockSpec(memory_space=pltpu.VMEM)
    out_shape = [jax.ShapeDtypeStruct((k, pieces * chunk), F32)]
    if final:
        out_shape.append(jax.ShapeDtypeStruct((k, LANES), F32))
    return pl.pallas_call(
        functools.partial(orth_kernel, axis, parts, other_axis, others, count, final),
        out_shape=out_shape,
        in_specs=[vmem, vmem],
        out_specs=[vmem] * len(out_shape),
        scratch_shapes=[
            pltpu.VMEM((slots, k, chunk), F32),
            pltpu.VMEM((pieces, k, chunk), F32),
            pltpu.VMEM((others, k * k // LANES, LANES), F32),
            pltpu.VMEM((others, (2 if final else 1) * k * k // LANES, LANES), F32),
            dma((slots,)),
            dma((slots,)),
            dma((slots,)),
            dma((slots,)),
            dma((others - 1,)),
            dma((others - 1,)),
            dma((others - 1,)),
            dma((others - 1,)),
        ],
        compiler_params=pltpu.CompilerParams(collective_id=ident, has_side_effects=True),
        name=f"orth_{ident}",
    )(partial, thresholds)


def chunk_of(size, parts):
    chunk = size // parts
    return chunk if chunk * parts == size and chunk % LANES == 0 else size


def solution(mesh):
    vox, var = mesh.shape["vox"], mesh.shape["var"]

    def per_device(cross, start, levels):
        rows, cols = cross.shape
        k = start.shape[0]
        nv, ng = rows * vox, cols * var
        thresholds = levels.astype(F32) / 1024.0
        thresholds = jnp.broadcast_to(thresholds[:, :, None], (2, k, LANES))
        row_chunk, col_chunk = chunk_of(rows, var), chunk_of(cols, vox)
        right_dirs = start
        for sweep in range(ITERS):
            final = sweep == ITERS - 1
            partial = left_pass(cross, right_dirs, row_chunk)
            left_dirs = orth_step(partial, thresholds[0], "var", var, "vox", vox, nv, 2 * sweep)[0]
            partial = right_pass(cross, left_dirs, col_chunk)
            outs = orth_step(
                partial, thresholds[1], "vox", vox, "var", var, ng, 2 * sweep + 1, final
            )
            right_dirs = outs[0]
        root = math.sqrt(nv * ng)
        strength = outs[1] / root
        deflated = deflate(cross, left_dirs, strength / root, right_dirs)
        return (deflated, left_dirs, right_dirs, strength[:, 0])

    in_specs = (P("vox", "var"), P(None, "var"), P())
    out_specs = (P("vox", "var"), P(None, "vox"), P(None, "var"), P())
    return jax.shard_map(
        per_device, mesh=mesh, in_specs=in_specs, out_specs=out_specs, check_vma=False
    )
```
